256 devices in a mesh: dp: 8 (over y, core), space: 32 (over z, x).
Axes of the slice: x: 4, y: 4, z: 8, core: 2. Of those that a mesh axis runs over, the one named last changes fastest.
Arguments:
- features: bfloat16 [8, 1024, 64, 512], P('dp', 'space'), may hold values from -50 to 50
- owners: int32 [8, 1024, 1], P('dp', 'space'), may hold values from 0 to 31; in each aligned block of 32 rows (0 to 31, 32 to 63, ..., all dimensions but the last counted through in order) at most 2 rows name the same one
- neighbors: int32 [8, 1024, 3], P('dp', 'space'), may hold values from -1 to 1022, as said below
- w_reduce: bfloat16 [512, 128], replicated, may hold values from -0.25 to 0.25
- w_spatial: bfloat16 [1152, 128], replicated, may hold values from -0.1875 to 0.1875
- w_expand: bfloat16 [128, 512], replicated, may hold values from -0.5 to 0.5
- w_short: bfloat16 [512, 512], replicated, may hold values from -0.25 to 0.25
- gains_mid: float32 [2, 128], replicated, may hold values from 0.25 to 1.75
- shifts_mid: float32 [2, 128], replicated, may hold values from -2.5 to 2.5
- gains_wide: float32 [2, 512], replicated, may hold values from 0.25 to 1.75
- shifts_wide: float32 [2, 512], replicated, may hold values from -2.5 to 2.5
- cotangent: bfloat16 [8, 2048, 16, 512], P('dp', 'space'), may hold values from -6 to 6
Outputs:
- block_out: bfloat16 [8, 2048, 16, 512], P('dp', 'space')
- grad_features: bfloat16 [8, 1024, 64, 512], P('dp', 'space')
- grad_reduce: float32 [512, 128], P('space')
- grad_spatial: float32 [1152, 128], P('space')
- grad_expand: float32 [128, 512], P('space')
- grad_short: float32 [512, 512], P('space')
- grad_gains_mid: float32 [2, 128], P(None, 'space')
- grad_shifts_mid: float32 [2, 128], P(None, 'space')
- grad_gains_wide: float32 [2, 512], P(None, 'space')
- grad_shifts_wide: float32 [2, 512], P(None, 'space')
The draws below stay inside these ranges and needn't reach their ends.
Inputs may be any that keep to these rules, and one draw needn't show every extreme that they name: `owners`: among the 32 tiles of one block no owner is named more than 2 times. `neighbors`: entries are tile indices of the same slide or -1 for none; for tile t every index lies between t - 32 and t - 1.
All inputs are finite; a program needn't handle non-finite values.
Results may differ from the reference program's by a relative error of at most 0.02.
Values may be sent and summed in bfloat16 or wider, within the bound.
No kernel may reach another device: no remote copies, remote signals or barrier semaphores. Data moves between devices by JAX's collectives and lax.ppermute only.
A program may use at most 64 MiB of HBM per device.

```python
import math
import jax
import jax.numpy as jnp
import numpy as np
from jax import lax

C_IN = 512
C_MID = 128
GROUPS = 32
SIDE = 8
TILE_DEV = 32
BLOCKS = 32
SLIDES = 8
TILES = 1024
CAP = 2
SLOTS = 2048


def draw_features(key, part):
    folded = jax.random.fold_in(key, 11)
    subkeys = jax.random.split(folded, 3)
    tile_place = jnp.arange(TILES, dtype=jnp.float32) / TILES
    tile_scale = jnp.exp(math.log(3.0) * tile_place[None, :] + jax.random.uniform(subkeys[0], (SLIDES, TILES), jnp.float32, 0.0, math.log(3.3)))
    chan_scale = jnp.exp(jax.random.uniform(subkeys[1], (C_IN,), jnp.float32, 0.0, math.log(10.0)))
    noise_draw = jnp.clip(jax.random.normal(subkeys[2], (SLIDES, TILES, SIDE * SIDE, C_IN), jnp.float32), -4.0, 4.0)
    values = noise_draw * tile_scale[:, :, None, None] * chan_scale / 8.0
    return values.astype(jnp.bfloat16)


def draw_neighbors(key, part):
    folded = jax.random.fold_in(key, 23)
    subkeys = jax.random.split(folded, 2)
    tile_ids = jnp.arange(TILES, dtype=jnp.int32)[None, :]
    step_up = jax.random.randint(subkeys[0], (SLIDES, TILES), 2, TILE_DEV, dtype=jnp.int32)
    step_up = jnp.where(tile_ids % 8 == 3, TILE_DEV - 1, step_up)
    upward = tile_ids - step_up
    leftward = jnp.broadcast_to(tile_ids - 1, (SLIDES, TILES))
    corner = upward - 1
    stacked = jnp.stack([upward, leftward, corner], axis=-1)
    kept_mask = jax.random.randint(subkeys[1], (SLIDES, TILES, 3), 0, 8, dtype=jnp.int32) != 0
    return jnp.where(kept_mask & (stacked >= 0), stacked, -1).astype(jnp.int32)


def draw_cotangent(key, part):
    folded = jax.random.fold_in(key, 37)
    subkeys = jax.random.split(folded, 4)
    quarter = SIDE // 2 * (SIDE // 2)
    full_shape = (SLIDES, SLOTS, quarter, C_IN)
    slide_sign = jnp.where(jax.random.uniform(subkeys[0], (SLIDES, 1, 1, 1), jnp.float32) < 0.5, -1.0, 1.0)
    channel_part = jnp.clip(jax.random.normal(subkeys[2], (SLIDES, 1, 1, C_IN), jnp.float32), -2.0, 2.0)
    common = slide_sign * jax.random.uniform(subkeys[1], (SLIDES, 1, 1, 1), jnp.float32, 0.5, 0.8)
    noise_draw = jnp.clip(jax.random.normal(subkeys[3], full_shape, jnp.float32), -4.0, 4.0)
    values = noise_draw + common + 0.6 * channel_part
    return jnp.clip(values, -6.0, 6.0).astype(jnp.bfloat16)


def shared_out(key, own, number, rows, amount, top, reach, lean):
    sequence = jax.random.permutation(key, amount)
    packed, ordinary = shares(amount, rows * top, reach, lean, True), shares(amount, rows * top, reach, lean, False)
    places = jnp.arange(amount)

    def named(tallies, rotation):
        used = int((tallies > 0).sum())
        fixed = max(1, used // 4)
        moved = fixed + (places - fixed + rotation * (used - fixed)) % max(1, amount - fixed)
        return jnp.zeros((amount,), jnp.int32).at[sequence[jnp.where(places < fixed, places, moved)]].set(jnp.asarray(tallies, jnp.int32))

    tallies = jnp.where(number % 4 == 0, named(packed, number // 4), named(ordinary, number - number // 4 - 1))
    mixed = jax.random.permutation(jax.random.fold_in(own, 3), amount)
    giver, taker = mixed[0:amount // 2 * 2:2], mixed[1:amount // 2 * 2:2]
    room = jnp.minimum(tallies[giver] - 1, reach - tallies[taker]) // 2
    room = jnp.where((giver == sequence[0]) | (taker == sequence[0]) | (tallies[taker] == 0), 0, jnp.maximum(room, 0))
    moved = jax.random.randint(jax.random.fold_in(own, 4), (amount // 2,), 0, 1 << 20) % (room + 1)
    tallies = tallies.at[giver].add(-moved).at[taker].add(moved)
    labels = jnp.searchsorted(jnp.cumsum(tallies), jnp.arange(rows * top), side="right").astype(jnp.int32)
    grid = labels.reshape(top, rows).T
    grid = grid[jax.random.permutation(jax.random.fold_in(own, 1), rows)]
    rotation = jax.random.randint(jax.random.fold_in(own, 2), (rows, 1), 0, top)
    return jnp.take_along_axis(grid, (jnp.arange(top)[None, :] + rotation) % top, axis=1)


def shares(amount, total, reach, skew, full):
    loads = [(1 << 20) // math.isqrt(rank ** skew) + 1 for rank in range(1, amount + 1)]
    largest = reach if full else min(reach, max(-(-total // amount), total * loads[0] // sum(loads)))
    least = 1 if total - largest >= amount - 1 else 0
    holding, rest = [largest] + [least] * (amount - 1), total - largest - least * (amount - 1)
    while rest > 0:
        movable = [i for i in range(1, amount) if holding[i] < largest] or [i for i in range(1, amount) if holding[i] < reach]
        whole, left = sum([loads[i] for i in movable]), rest
        for i in movable:
            extra = min(reach - holding[i], max(1, left * loads[i] // whole), rest)
            holding[i] = holding[i] + extra
            rest = rest - extra
    return np.array(holding)


def scatter_about(rng, extent, deviation, most, held_as=jnp.bfloat16):
    entries = jax.random.normal(rng, extent, jnp.float32) * deviation
    return jnp.minimum(jnp.maximum(entries, -most), most).astype(held_as)


def setup_inputs(seed: int = 0) -> dict:
    key_of = jax.random.split(jax.random.key(seed), 13)
    features = draw_features(jax.random.fold_in(key_of[12], 71), 0)
    owners_keys = jax.random.split(jax.random.fold_in(key_of[1], 1), SLIDES * TILES // TILE_DEV)
    owners_turns = jax.random.permutation(jax.random.fold_in(key_of[1], 3), SLIDES * TILES // TILE_DEV)
    owners = jax.vmap(lambda own, number: shared_out(jax.random.fold_in(key_of[1], 2), own, number, TILE_DEV, BLOCKS, 1, CAP, 2))(owners_keys, owners_turns).reshape((SLIDES, TILES, 1))
    neighbors = draw_neighbors(jax.random.fold_in(key_of[12], 71), 0)
    w_reduce = scatter_about(key_of[3], (C_IN, C_MID), C_IN ** -0.5, 0.25)
    w_spatial = scatter_about(key_of[4], (9 * C_MID, C_MID), (9 * C_MID) ** -0.5, 0.1875)
    w_expand = scatter_about(key_of[5], (C_MID, C_IN), C_MID ** -0.5, 0.5)
    w_short = scatter_about(key_of[6], (C_IN, C_IN), C_IN ** -0.5, 0.25)
    gains_mid = jnp.clip(1.0 + 0.15 * jax.random.normal(key_of[7], (2, C_MID), jnp.float32), 0.25, 1.75)
    shifts_mid = scatter_about(key_of[8], (2, C_MID), 0.5, 2.5, jnp.float32)
    gains_wide = jnp.clip(1.0 + 0.15 * jax.random.normal(key_of[9], (2, C_IN), jnp.float32), 0.25, 1.75)
    shifts_wide = scatter_about(key_of[10], (2, C_IN), 0.5, 2.5, jnp.float32)
    cotangent = draw_cotangent(jax.random.fold_in(key_of[12], 71), 0)
    return dict(features=features, owners=owners, neighbors=neighbors, w_reduce=w_reduce, w_spatial=w_spatial, w_expand=w_expand, w_short=w_short, gains_mid=gains_mid, shifts_mid=shifts_mid, gains_wide=gains_wide, shifts_wide=shifts_wide, cotangent=cotangent)


EPS = 1e-05

def smooth(values):
    return values * jax.nn.sigmoid(values)

def smooth_slope(values):
    sig = jax.nn.sigmoid(values)
    return sig * (1.0 + values * (1.0 - sig))

def group_total(per_channel):
    width = per_channel.shape[-1]
    grouped = per_channel.reshape(per_channel.shape[:-1] + (GROUPS, width // GROUPS))
    return jnp.repeat(lax.optimization_barrier(jnp.sum(grouped, axis=-1)), width // GROUPS, axis=-1)

def moments(conv_out):
    values = conv_out.astype(jnp.float32)
    return jnp.stack([lax.optimization_barrier(jnp.sum(values, axis=0)), lax.optimization_barrier(jnp.sum(values * values, axis=0))])

def grad_moments(upstream, normed):
    return jnp.stack([lax.optimization_barrier(jnp.sum(upstream, axis=0)), lax.optimization_barrier(jnp.sum(upstream * normed, axis=0))])

def norm_forward(conv_out, totals, members, gain_row, shift_row):
    center = group_total(totals[0]) / members
    spread = group_total(totals[1]) / members - center * center
    inv_spread = lax.rsqrt(spread + EPS)
    normed = (conv_out.astype(jnp.float32) - center) * inv_spread
    return (normed, normed * gain_row + shift_row, center, inv_spread)

def norm_backward(upstream, normed, inv_spread, gain_row, totals, members):
    first = group_total(gain_row * totals[0]) / members
    second = group_total(gain_row * totals[1]) / members
    return inv_spread * (gain_row * upstream - first - normed * second)

def slide_pass(tile_feats, owner_of, links, w_reduce, w_spatial, w_expand, w_short, gains_mid, shifts_mid, gains_wide, shifts_wide, cot_slide):
    half = SIDE // 2
    quarter = half * half
    members_in = TILES * SIDE * SIDE * (C_MID // GROUPS)
    members_mid = TILES * quarter * (C_MID // GROUPS)
    members_wide = TILES * quarter * (C_IN // GROUPS)
    flat_in = tile_feats.reshape(TILES * SIDE * SIDE, C_IN)
    conv_one = jnp.dot(flat_in, w_reduce, preferred_element_type=jnp.float32).astype(jnp.bfloat16)
    normed_one, pre_one, center_one, scale_one = norm_forward(conv_one, moments(conv_one), members_in, gains_mid[0], shifts_mid[0])
    act_one = smooth(pre_one).astype(jnp.bfloat16)
    safe_links = jnp.where(links < 0, TILES, links).astype(jnp.int32)
    grid_act = act_one.reshape(TILES, SIDE, SIDE, C_MID)
    blank = jnp.zeros((1, SIDE, C_MID), jnp.bfloat16)
    row_ext = jnp.concatenate([grid_act[:, SIDE - 1], blank], axis=0)
    col_ext = jnp.concatenate([grid_act[:, :, SIDE - 1], blank], axis=0)
    top_row = row_ext[safe_links[:, 0]]
    left_col = col_ext[safe_links[:, 1]]
    corner_cell = row_ext[safe_links[:, 2], SIDE - 1]
    first_line = jnp.concatenate([corner_cell[:, None], top_row], axis=1)
    lower_rows = jnp.concatenate([left_col[:, :, None], grid_act], axis=2)
    padded = jnp.concatenate([first_line[:, None], lower_rows], axis=1)
    columns = jnp.concatenate([padded[:, offset_row:offset_row + SIDE - 1:2, offset_col:offset_col + SIDE - 1:2] for offset_row in range(3) for offset_col in range(3)], axis=-1).reshape(TILES * quarter, 9 * C_MID)
    conv_two = jnp.dot(columns, w_spatial, preferred_element_type=jnp.float32).astype(jnp.bfloat16)
    normed_two, pre_two, center_two, scale_two = norm_forward(conv_two, moments(conv_two), members_mid, gains_mid[1], shifts_mid[1])
    act_two = smooth(pre_two).astype(jnp.bfloat16)
    conv_three = jnp.dot(act_two, w_expand, preferred_element_type=jnp.float32).astype(jnp.bfloat16)
    sub_in = tile_feats.reshape(TILES, SIDE, SIDE, C_IN)[:, ::2, ::2].reshape(TILES * quarter, C_IN)
    conv_short = jnp.dot(sub_in, w_short, preferred_element_type=jnp.float32).astype(jnp.bfloat16)
    normed_three, pre_three, center_three, scale_three = norm_forward(conv_three, moments(conv_three), members_wide, gains_wide[0], shifts_wide[0])
    normed_short, pre_short, center_short, scale_short = norm_forward(conv_short, moments(conv_short), members_wide, gains_wide[1], shifts_wide[1])
    summed = pre_three + pre_short
    result = smooth(summed).astype(jnp.bfloat16)
    owner_hits = (owner_of[:, None] == jnp.arange(BLOCKS, dtype=jnp.int32)[None, :]).astype(jnp.int32).reshape(BLOCKS, TILE_DEV, BLOCKS)
    before = jnp.cumsum(owner_hits, axis=1) - owner_hits
    rank_in = lax.optimization_barrier(jnp.sum(before * owner_hits, axis=2)).reshape(TILES).astype(jnp.int32)
    source = jnp.arange(TILES, dtype=jnp.int32) // TILE_DEV
    slot_of = (owner_of * (BLOCKS * CAP) + source * CAP + rank_in).astype(jnp.int32)
    out_slide = jnp.zeros((SLOTS, quarter, C_IN), jnp.bfloat16).at[slot_of].set(result.reshape(TILES, quarter, C_IN))
    picked = cot_slide[slot_of].reshape(TILES * quarter, C_IN).astype(jnp.float32)
    upstream = picked * smooth_slope(summed)
    totals_three = grad_moments(upstream, normed_three)
    totals_short = grad_moments(upstream, normed_short)
    dconv_three = norm_backward(upstream, normed_three, scale_three, gains_wide[0], totals_three, members_wide).astype(jnp.bfloat16)
    dconv_short = norm_backward(upstream, normed_short, scale_short, gains_wide[1], totals_short, members_wide).astype(jnp.bfloat16)
    grad_expand_part = jnp.dot(act_two.T, dconv_three, preferred_element_type=jnp.float32)
    grad_short_part = jnp.dot(sub_in.T, dconv_short, preferred_element_type=jnp.float32)
    back_two = jnp.dot(dconv_three, w_expand.T, preferred_element_type=jnp.float32)
    back_two = back_two * smooth_slope(pre_two)
    totals_two = grad_moments(back_two, normed_two)
    dconv_two = norm_backward(back_two, normed_two, scale_two, gains_mid[1], totals_two, members_mid).astype(jnp.bfloat16)
    grad_spatial_part = jnp.dot(columns.T, dconv_two, preferred_element_type=jnp.float32)
    back_cols = jnp.dot(dconv_two, w_spatial.T, preferred_element_type=jnp.float32).reshape(TILES, half, half, 9, C_MID)
    back_pad = jnp.zeros((TILES, SIDE + 1, SIDE + 1, C_MID), jnp.float32)
    for offset_row in range(3):
        for offset_col in range(3):
            back_pad = back_pad.at[:, offset_row:offset_row + SIDE - 1:2, offset_col:offset_col + SIDE - 1:2].add(back_cols[:, :, :, 3 * offset_row + offset_col])
    rows_acc = jnp.zeros((TILES + 1, SIDE, C_MID), jnp.float32).at[safe_links[:, 0]].add(back_pad[:, 0, 1:])
    rows_acc = rows_acc.at[safe_links[:, 2], SIDE - 1].add(back_pad[:, 0, 0])
    cols_acc = jnp.zeros((TILES + 1, SIDE, C_MID), jnp.float32).at[safe_links[:, 1]].add(back_pad[:, 1:, 0])
    inner = back_pad[:, 1:, 1:]
    inner = inner.at[:, SIDE - 1].add(rows_acc[:TILES]).at[:, :, SIDE - 1].add(cols_acc[:TILES])
    back_one = (inner * smooth_slope(pre_one).reshape(TILES, SIDE, SIDE, C_MID)).reshape(TILES * SIDE * SIDE, C_MID)
    totals_one = grad_moments(back_one, normed_one)
    dconv_one = norm_backward(back_one, normed_one, scale_one, gains_mid[0], totals_one, members_in).astype(jnp.bfloat16)
    grad_reduce_part = jnp.dot(flat_in.T, dconv_one, preferred_element_type=jnp.float32)
    back_in = jnp.dot(dconv_one, w_reduce.T, preferred_element_type=jnp.float32).reshape(TILES, SIDE, SIDE, C_IN)
    back_short = jnp.dot(dconv_short, w_short.T, preferred_element_type=jnp.float32).reshape(TILES, half, half, C_IN)
    back_in = back_in.at[:, ::2, ::2].add(back_short)
    grad_feat = back_in.reshape(TILES, SIDE * SIDE, C_IN).astype(jnp.bfloat16)
    partials = (grad_reduce_part, grad_spatial_part, grad_expand_part, grad_short_part, jnp.stack([totals_one[1], totals_two[1]]), jnp.stack([totals_one[0], totals_two[0]]), jnp.stack([totals_three[1], totals_short[1]]), jnp.stack([totals_three[0], totals_short[0]]))
    return (out_slide, grad_feat, partials)

def reference(features, owners, neighbors, w_reduce, w_spatial, w_expand, w_short, gains_mid, shifts_mid, gains_wide, shifts_wide, cotangent):
    out_list = []
    grad_list = []
    running = None
    for slide in range(SLIDES):
        out_slide, grad_feat, partials = slide_pass(features[slide], owners[slide, :, 0], neighbors[slide], w_reduce, w_spatial, w_expand, w_short, gains_mid, shifts_mid, gains_wide, shifts_wide, cotangent[slide])
        out_list.append(out_slide)
        grad_list.append(grad_feat)
        if running is None:
            running = partials
        else:
            running = jax.tree.map(jnp.add, running, partials)
    scale_in = 1.0 / math.sqrt(SLIDES * TILES * SIDE * SIDE)
    scale_out = 1.0 / math.sqrt(SLIDES * TILES * (SIDE // 2) * (SIDE // 2))
    mid_scale = jnp.array([[scale_in], [scale_out]], jnp.float32)
    return (jnp.stack(out_list), jnp.stack(grad_list), running[0] * scale_in, running[1] * scale_out, running[2] * scale_out, running[3] * scale_out, running[4] * mid_scale, running[5] * mid_scale, running[6] * scale_out, running[7] * scale_out)
```

```python
import functools
import math

import jax
import jax.numpy as jnp
from jax import lax
from jax.experimental import pallas as pl
from jax.experimental.pallas import tpu as pltpu
from jax.sharding import PartitionSpec as P

GROUPS = 32
SIDE = 8
HALF = SIDE // 2
QUARTER = HALF * HALF
POSITIONS = SIDE * SIDE
LANES = 128
EPS = 1e-05
F32 = jnp.float32
BF16 = jnp.bfloat16
I32 = jnp.int32
STAT_ROW = 128
HALF_ROWS = 64
SUM_ROWS = HALF_ROWS + 16
RIMS = [(SIDE - 1) * SIDE + c for c in range(SIDE)] + [r * SIDE + SIDE - 1 for r in range(SIDE)]


def struct(shape, dtype):
    return jax.ShapeDtypeStruct(shape, dtype)


def far(shape, dtype):
    return pltpu.HBM(shape, dtype)


def small_grant():
    return pltpu.CompilerParams(vmem_limit_bytes=24 << 20)


def held(array):
    return pltpu.with_memory_space_constraint(array, pltpu.HBM)


def whole(shape):
    return pl.BlockSpec(tuple(shape), lambda g: (0,) * len(shape))


def run(kernel, outs, args, scratch=(), scalars=(), specs=None, near=()):
    specs = specs or {}
    args = [arg if k in near or k in scalars else held(arg) for k, arg in enumerate(args)]
    smem = pl.BlockSpec(memory_space=pltpu.SMEM)
    in_specs = [
        smem if k in scalars else specs.get(k) or whole(arg.shape) for k, arg in enumerate(args)
    ]
    return pl.pallas_call(
        kernel,
        grid=(1,),
        out_shape=outs,
        in_specs=in_specs,
        out_specs=[whole(out.shape) for out in outs],
        scratch_shapes=list(scratch),
        compiler_params=small_grant(),
    )(*args)


def lane_of(shape):
    return lax.broadcasted_iota(I32, shape, len(shape) - 1)


def row_of(shape):
    return lax.broadcasted_iota(I32, shape, len(shape) - 2)


def onehot(mask, dtype=BF16):
    return jnp.where(mask, 1.0, 0.0).astype(dtype)


def exact_dot(a, b, dims):
    return lax.dot_general(
        a, b, (dims, ((), ())), precision=lax.Precision.HIGHEST, preferred_element_type=F32
    )


def dot(a, b, dims=((1,), (0,))):
    return lax.dot_general(a, b, (dims, ((), ())), preferred_element_type=F32)


def group_matrix(width):
    shift = (width // GROUPS).bit_length() - 1
    shape = (width, LANES)
    return onehot((row_of(shape) >> shift) == (lane_of(shape) & (GROUPS - 1)), F32)


def lane_blocks():
    shape = (8, LANES)
    return (lane_of(shape) >> 5) == row_of(shape)


def rows8(rows):
    shape = (8, rows[0].shape[-1])
    place = row_of(shape)
    total = jnp.zeros(shape, F32)
    for k, row in enumerate(rows):
        total = jnp.where(place == k, jnp.broadcast_to(row, shape), total)
    return total


def group_line(rows):
    groups = exact_dot(rows, group_matrix(rows.shape[-1]), ((1,), (0,)))
    return jnp.sum(jnp.where(lane_blocks(), groups, 0.0), axis=0, keepdims=True)


def pack(rows, out_ref):
    line = group_line(rows)
    out_ref[...] = jnp.broadcast_to(line.reshape(1, 1, LANES), out_ref.shape)


def pack_thin(rows, out_ref):
    line = group_line(rows)
    high = line.astype(BF16).astype(F32)
    middle = (line - high).astype(BF16).astype(F32)
    low = line - high - middle
    block = rows8([high, middle, low]).astype(BF16)
    shape = (out_ref.shape[0], 8, LANES)
    out_ref[:, STAT_ROW : STAT_ROW + 8, :] = jnp.broadcast_to(block[None], shape)


def unpack(in_ref, width):
    if len(in_ref.shape) == 3 and in_ref.shape[1] == 8:
        line = column_sum(jnp.sum(in_ref[...].astype(F32), axis=0))
    else:
        line = jnp.sum(in_ref[...], axis=0)
    spread = jnp.where(lane_blocks(), jnp.broadcast_to(line, (8, LANES)), 0.0)
    return exact_dot(spread, group_matrix(width), ((1,), (1,)))


def center_scale(total, square, members):
    center = total / members
    spread = square / members - center * center
    return center, lax.rsqrt(spread + EPS)


def column_sum(values):
    return jnp.sum(values, axis=0, keepdims=True)


def gate(values):
    return 1.0 / (1.0 + jnp.exp(-values))


def smooth(values):
    return values * gate(values)


def smooth_slope(values):
    sig = gate(values)
    return sig * (1.0 + values * (1.0 - sig))


def stack_lanes(values, out_ref, rows):
    high = values.shape[1]
    for j in range(values.shape[2] // LANES):
        out_ref[rows, j * high : (j + 1) * high, :] = values[:, :, j * LANES : (j + 1) * LANES]


def reduce_kernel(f_ref, w_ref, cot_ref, c1_ref, rim_ref, s_ref, flat, acc):
    step = pl.program_id(0)
    peers = cot_ref.shape[0]
    stack_lanes(cot_ref[...], s_ref, pl.ds(step * peers, peers))
    tiles = f_ref.shape[0] // POSITIONS
    conv = dot(f_ref[...], w_ref[...]).astype(BF16).astype(F32)
    flat[...] = conv

    @pl.when(step == 0)
    def _():
        acc[...] = jnp.zeros(acc.shape, F32)

    acc[...] += rows8([column_sum(conv), column_sum(conv * conv)])
    for p in range(POSITIONS):
        c1_ref[p] = flat[pl.ds(p, tiles, stride=POSITIONS), :].astype(BF16)
    for k, p in enumerate(RIMS):
        rim_ref[k] = c1_ref[p]

    @pl.when(step == pl.num_programs(0) - 1)
    def _():
        pack_thin(acc[...], s_ref)


def pick_rows(shape, across):
    out, src = (row_of(shape), lane_of(shape)) if not across else (lane_of(shape), row_of(shape))
    q = out & (QUARTER - 1)
    place = ((out >> 4) << 6) + ((q >> 2) << 4) + ((q & 3) << 1)
    return onehot(place == src)


def short_kernel(f_ref, w_ref, sub_ref, cs_ref, ms_ref):
    step = pl.program_id(0)
    picked = pick_rows((4 * QUARTER, 4 * POSITIONS), False)
    for g in range(f_ref.shape[0] // (4 * POSITIONS)):
        block = f_ref[g * 4 * POSITIONS : (g + 1) * 4 * POSITIONS, :]
        sub_ref[g * 4 * QUARTER : (g + 1) * 4 * QUARTER, :] = dot(picked, block).astype(BF16)
    conv = dot(sub_ref[...], w_ref[...]).astype(BF16)
    cs_ref[...] = conv
    conv = conv.astype(F32)

    @pl.when(step == 0)
    def _():
        ms_ref[...] = jnp.zeros(ms_ref.shape, F32)

    zero = jnp.zeros((1, conv.shape[1]), F32)
    ms_ref[...] += rows8([zero, zero, column_sum(conv), column_sum(conv * conv)])


def spatial_kernel(
    members, c1_ref, prior_ref, g_ref, link_ref, gain_ref, shift_ref, w_ref, c2_ref, col_ref, v_ref, s_ref, act
):
    tiles = c1_ref.shape[1]
    width = c1_ref.shape[2]
    totals = unpack(g_ref, width)
    center, scale = center_scale(totals[0:1], totals[1:2], members)
    v_ref[...] = rows8([center, scale])
    gain, shift = gain_ref[0:1, :], shift_ref[0:1, :]
    factor = scale * gain
    offset = shift - center * factor

    def activated(raw):
        return smooth(raw.astype(F32) * factor + offset).astype(BF16)

    for p in range(POSITIONS):
        act[p] = activated(c1_ref[p])
    pool = [
        jnp.concatenate([activated(prior_ref[k]), act[p]], axis=0) for k, p in enumerate(RIMS)
    ]
    slots = lane_of((tiles, 2 * tiles))

    def chosen(column, parts):
        match = onehot(link_ref[:, column : column + 1] == slots)
        return dot(match, jnp.concatenate(parts, axis=1)).astype(BF16)

    top = chosen(0, pool[:SIDE])
    left = chosen(1, pool[SIDE:])
    corner = chosen(2, pool[SIDE - 1 : SIDE])

    def padded(row, col):
        if row == 0 and col == 0:
            return corner
        if row == 0:
            return top[:, (col - 1) * width : col * width]
        if col == 0:
            return left[:, (row - 1) * width : row * width]
        return act[(row - 1) * SIDE + col - 1]

    for i in range(HALF):
        for j in range(HALF):
            q = i * HALF + j
            for k in range(9):
                col_ref[q * tiles : (q + 1) * tiles, k * width : (k + 1) * width] = padded(
                    2 * i + k // 3, 2 * j + k % 3
                )
    conv = dot(col_ref[...], w_ref[...]).astype(BF16)
    c2_ref[...] = conv
    conv = conv.astype(F32)
    pack(rows8([column_sum(conv), column_sum(conv * conv)]), s_ref)


def expand_kernel(
    members, c2_ref, g_ref, gain_ref, shift_ref, w_ref, ms_ref, act_ref, c3_ref, v_ref, s_ref, flat
):
    width = c2_ref.shape[1]
    tiles = c2_ref.shape[0] // QUARTER
    totals = unpack(g_ref, width)
    center, scale = center_scale(totals[0:1], totals[1:2], members)
    v_ref[...] = rows8([center, scale])
    normed = (c2_ref[...].astype(F32) - center) * scale
    flat[...] = smooth(normed * gain_ref[1:2, :] + shift_ref[1:2, :])
    for t in range(tiles):
        act_ref[t * QUARTER : (t + 1) * QUARTER, :] = flat[pl.ds(t, QUARTER, stride=tiles), :].astype(
            BF16
        )
    conv = dot(act_ref[...], w_ref[...]).astype(BF16)
    c3_ref[...] = conv
    conv = conv.astype(F32)
    pack(rows8([column_sum(conv), column_sum(conv * conv)]) + ms_ref[...], s_ref)


def join_kernel(
    members,
    capacity,
    owner_ref,
    c3_ref,
    cs_ref,
    g_ref,
    gain_ref,
    shift_ref,
    cot_ref,
    out_ref,
    up_ref,
    v_ref,
    sum_ref,
    counts,
    slots,
):
    width = c3_ref.shape[1]
    tiles = owner_ref.shape[0]

    def clear(k, carry):
        counts[k] = 0
        return carry

    lax.fori_loop(0, counts.shape[0], clear, 0)

    def place(t, carry):
        owner = owner_ref[t]
        rank = counts[owner]
        counts[owner] = rank + 1
        slots[t] = rank
        return carry

    lax.fori_loop(0, tiles, place, 0)
    totals = unpack(g_ref, width)
    center_three, scale_three = center_scale(totals[0:1], totals[1:2], members)
    center_short, scale_short = center_scale(totals[2:3], totals[3:4], members)
    v_ref[...] = rows8([center_three, scale_three, center_short, scale_short])
    gain_three, gain_short = gain_ref[0:1, :], gain_ref[1:2, :]
    shift = shift_ref[0:1, :] + shift_ref[1:2, :]
    out_ref[:, 0:STAT_ROW, :] = jnp.zeros((out_ref.shape[0], STAT_ROW, LANES), BF16)
    high = capacity * QUARTER

    def fold(values):
        return values[:8] + values[8:]

    def tile(t, sums):
        rows = pl.ds(pl.multiple_of(t * QUARTER, QUARTER), QUARTER)
        owner = owner_ref[t]
        start = pl.multiple_of(slots[t] * QUARTER, QUARTER)
        three = (c3_ref[rows, :].astype(F32) - center_three) * scale_three
        short = (cs_ref[rows, :].astype(F32) - center_short) * scale_short
        summed = three * gain_three + short * gain_short + shift
        sig = gate(summed)
        result = (summed * sig).astype(BF16)
        picked = []
        for j in range(width // LANES):
            place = pl.ds(j * high + start, QUARTER)
            out_ref[owner, place, :] = result[:, j * LANES : (j + 1) * LANES]
            picked.append(cot_ref[owner, place, :])
        upstream = jnp.concatenate(picked, axis=1).astype(F32) * (sig * (1.0 + summed * (1.0 - sig)))
        up_ref[rows, :] = upstream
        return (
            sums[0] + fold(upstream),
            sums[1] + fold(upstream * three),
            sums[2] + fold(upstream * short),
        )

    zero = jnp.zeros((8, width), F32)
    sums = lax.fori_loop(0, tiles, tile, (zero, zero, zero))
    up, three, short = (column_sum(part) for part in sums)
    sum_ref[...] = rows8([three, short, up])
    pack_thin(
        rows8([gain_three * up, gain_three * three, gain_short * up, gain_short * short]), out_ref
    )


def unstack_kernel(in_ref, out_ref):
    high = in_ref.shape[1] * LANES // out_ref.shape[2]
    shape = (out_ref.shape[0], out_ref.shape[1], LANES)
    for j in range(out_ref.shape[2] // LANES):
        part = in_ref[:, j * high : (j + 1) * high, :]
        out_ref[:, :, j * LANES : (j + 1) * LANES] = part.reshape(shape)


def back_two_kernel(
    members,
    c3_ref,
    cs_ref,
    up_ref,
    vw_ref,
    g_ref,
    gain_ref,
    c2_ref,
    v2_ref,
    gain_mid_ref,
    shift_mid_ref,
    w_ref,
    d3_ref,
    ds_ref,
    b2_ref,
    sum_ref,
    s_ref,
    flat,
):
    width = c3_ref.shape[1]
    tiles = c3_ref.shape[0] // QUARTER
    totals = unpack(g_ref, width) / members
    center_three, scale_three = vw_ref[0:1, :], vw_ref[1:2, :]
    center_short, scale_short = vw_ref[2:3, :], vw_ref[3:4, :]
    gain_three, gain_short = gain_ref[0:1, :], gain_ref[1:2, :]
    chunk = 64

    def block(k, carry):
        rows = pl.ds(pl.multiple_of(k * chunk, chunk), chunk)
        up = up_ref[rows, :]
        three = (c3_ref[rows, :].astype(F32) - center_three) * scale_three
        short = (cs_ref[rows, :].astype(F32) - center_short) * scale_short
        d3_ref[rows, :] = (
            scale_three * (gain_three * up - totals[0:1] - three * totals[1:2])
        ).astype(BF16)
        ds_ref[rows, :] = (
            scale_short * (gain_short * up - totals[2:3] - short * totals[3:4])
        ).astype(BF16)
        return carry

    lax.fori_loop(0, c3_ref.shape[0] // chunk, block, 0)
    flat[...] = dot(d3_ref[...], w_ref[...], ((1,), (1,)))
    center, scale = v2_ref[0:1, :], v2_ref[1:2, :]
    gain, shift = gain_mid_ref[1:2, :], shift_mid_ref[1:2, :]
    first = jnp.zeros((tiles, flat.shape[1]), F32)
    second = first
    for q in range(QUARTER):
        rows = slice(q * tiles, (q + 1) * tiles)
        normed = (c2_ref[rows, :].astype(F32) - center) * scale
        back = flat[pl.ds(q, tiles, stride=QUARTER), :] * smooth_slope(normed * gain + shift)
        b2_ref[rows, :] = back
        first = first + back
        second = second + back * normed
    first, second = column_sum(first), column_sum(second)
    sum_ref[...] = rows8([first, second])
    pack(rows8([gain * first, gain * second]), s_ref)


def wide_grads_kernel(act_ref, d3_ref, sub_ref, ds_ref, w_ref, ge_ref, gs_ref, bs_ref):
    ge_ref[...] = dot(act_ref[...], d3_ref[...], ((0,), (0,))).astype(BF16)
    gs_ref[...] = dot(sub_ref[...], ds_ref[...], ((0,), (0,))).astype(BF16)
    bs_ref[...] = dot(ds_ref[...], w_ref[...], ((1,), (1,))).astype(BF16)


def back_one_kernel(
    members,
    b2_ref,
    c2_ref,
    v2_ref,
    g_ref,
    gain_ref,
    shift_ref,
    w_ref,
    c1_ref,
    prior_ref,
    v1_ref,
    link_ref,
    d2_ref,
    b1_ref,
    rim_ref,
    sum_ref,
    s_ref,
    taps,
    own,
):
    tiles = c1_ref.shape[1]
    width = c1_ref.shape[2]
    totals = unpack(g_ref, width) / members
    center, scale = v2_ref[0:1, :], v2_ref[1:2, :]
    normed = (c2_ref[...].astype(F32) - center) * scale
    d2_ref[...] = (
        scale * (gain_ref[1:2, :] * b2_ref[...] - totals[0:1] - normed * totals[1:2])
    ).astype(BF16)
    for k in range(9):
        taps[k] = dot(d2_ref[...], w_ref[k * width : (k + 1) * width, :], ((1,), (1,))).reshape(
            QUARTER, tiles, width
        )

    def pad_sum(row, col):
        total = None
        for a in range(3):
            for b in range(3):
                if (row - a) % 2 or (col - b) % 2:
                    continue
                i, j = (row - a) // 2, (col - b) // 2
                if 0 <= i < HALF and 0 <= j < HALF:
                    part = taps[3 * a + b, i * HALF + j]
                    total = part if total is None else total + part
        return total

    slots = row_of((2 * tiles, tiles))

    def returned(column, parts):
        match = onehot(link_ref[column : column + 1, :] == slots)
        values = jnp.concatenate(parts, axis=1)
        high = values.astype(BF16)
        low = (values - high.astype(F32)).astype(BF16)
        return dot(match, high) + dot(match, low)

    rows = returned(0, [pad_sum(0, 1 + c) for c in range(SIDE)])
    cols = returned(1, [pad_sum(1 + r, 0) for r in range(SIDE)])
    corner = returned(2, [pad_sum(0, 0)])
    center, scale = v1_ref[0:1, :], v1_ref[1:2, :]
    gain, shift = gain_ref[0:1, :], shift_ref[0:1, :]
    first = jnp.zeros((tiles, width), F32)
    second = first
    for k in range(2 * SIDE):
        source = rows if k < SIDE else cols
        place = k % SIDE
        values = source[:, place * width : (place + 1) * width]
        if k == SIDE - 1:
            values = values + corner
        going = values[:tiles].astype(BF16)
        rim_ref[k] = going
        own[k] = values[tiles:]
        normed = (prior_ref[k].astype(F32) - center) * scale
        away = going.astype(F32) * smooth_slope(normed * gain + shift)
        first = first + away
        second = second + away * normed
    for p in range(POSITIONS):
        row, col = p // SIDE, p % SIDE
        total = pad_sum(row + 1, col + 1)
        if row == SIDE - 1:
            total = total + own[col]
        if col == SIDE - 1:
            total = total + own[SIDE + row]
        normed = (c1_ref[p].astype(F32) - center) * scale
        back = total * smooth_slope(normed * gain + shift)
        b1_ref[p * tiles : (p + 1) * tiles, :] = back
        first = first + back
        second = second + back * normed
    first, second = column_sum(first), column_sum(second)
    sum_ref[...] = rows8([first, second])
    pack(rows8([gain * first, gain * second]), s_ref)


def mid_grads_kernel(
    core_ref, col_ref, d2_ref, ge_ref, gs_ref, wide_ref, two_ref, one_ref, keep_ref, send_ref, flat, blocks, packed
):
    spaces = keep_ref.shape[0]
    width = d2_ref.shape[1]
    share = col_ref.shape[1] // spaces
    flat[0 : col_ref.shape[1], :] = dot(d2_ref[...], col_ref[...], ((0,), (0,))).T
    blocks[...] = jnp.zeros(blocks.shape, F32)

    def spread(row, per, start):
        shape = (spaces, row.shape[1])
        shift = per.bit_length() - 1
        kept = jnp.where((lane_of(shape) >> shift) == row_of(shape), jnp.broadcast_to(row, shape), 0.0)
        shape = (row.shape[1], LANES)
        return dot(
            kept.astype(BF16), onehot((row_of(shape) & (per - 1)) + start == lane_of(shape))
        )

    wide_share = wide_ref.shape[1] // spaces
    mid_share = width // spaces
    line = jnp.zeros((spaces, LANES), F32)
    for k in range(3):
        line = line + spread(wide_ref[k : k + 1, :], wide_share, k * wide_share)
    start = 3 * wide_share
    for k in range(2):
        line = line + spread(one_ref[k : k + 1, :], mid_share, start + 2 * k * mid_share)
        line = line + spread(two_ref[k : k + 1, :], mid_share, start + (2 * k + 1) * mid_share)
    for s in range(spaces):
        blocks[s, 0:share, :] = flat[s * share : (s + 1) * share, :]
        blocks[s, share : share + 1, :] = line[s : s + 1, :]
    shape = (spaces * 16, 4 * ge_ref.shape[0])
    out_row, src = row_of(shape), lane_of(shape)
    wanted = ((out_row >> 4) << 2) + (out_row & 3) + (((out_row & 15) >> 2) << 7)
    parts = jnp.concatenate([ge_ref[:, j * LANES : (j + 1) * LANES] for j in range(4)], axis=0)
    packed[:, 0:16, :] = dot(onehot(wanted == src), parts).astype(BF16).reshape(spaces, 16, LANES)
    for j in range(4):
        packed[:, 16 + 16 * j : 32 + 16 * j, :] = gs_ref[:, j * LANES : (j + 1) * LANES].reshape(
            spaces, 16, LANES
        )
    packed[:, 80:128, :] = blocks[...].astype(BF16)
    mine = pl.multiple_of(core_ref[0] * HALF_ROWS, HALF_ROWS)
    keep_ref[...] = packed[:, pl.ds(mine, HALF_ROWS), :]
    send_ref[...] = packed[:, pl.ds(HALF_ROWS - mine, HALF_ROWS), :]


def first_grad_kernel(
    members, b1_ref, c1_ref, rim_ref, v1_ref, g_ref, gain_ref, shift_ref, f_ref, keep_ref, twin_ref, d1_ref, out_ref, flat
):
    tiles = c1_ref.shape[1]
    width = c1_ref.shape[2]
    spaces = out_ref.shape[0]
    totals = unpack(g_ref, width) / members
    center, scale = v1_ref[0:1, :], v1_ref[1:2, :]
    gain, shift = gain_ref[0:1, :], shift_ref[0:1, :]
    for p in range(POSITIONS):
        row, col = p // SIDE, p % SIDE
        normed = (c1_ref[p].astype(F32) - center) * scale
        back = b1_ref[p * tiles : (p + 1) * tiles, :]
        arriving = None
        if row == SIDE - 1:
            arriving = rim_ref[col].astype(F32)
        if col == SIDE - 1:
            more = rim_ref[SIDE + row].astype(F32)
            arriving = more if arriving is None else arriving + more
        if arriving is not None:
            back = back + arriving * smooth_slope(normed * gain + shift)
        flat[p * tiles : (p + 1) * tiles, :] = scale * (
            gain * back - totals[0:1] - normed * totals[1:2]
        )
    for t in range(tiles):
        d1_ref[t * POSITIONS : (t + 1) * POSITIONS, :] = flat[
            pl.ds(t, POSITIONS, stride=tiles), :
        ].astype(BF16)
    grad = dot(d1_ref[...], f_ref[...], ((0,), (0,))).T
    share = grad.shape[0] // spaces
    out_ref[:, 0:HALF_ROWS, :] = (keep_ref[...].astype(F32) + twin_ref[...].astype(F32)).astype(BF16)
    out_ref[:, HALF_ROWS:SUM_ROWS, :] = grad.astype(BF16).reshape(spaces, share, width)


def features_kernel(d1_ref, w_ref, bs_ref, out_ref):
    back = dot(d1_ref[...], w_ref[...], ((1,), (1,)))
    spread = pick_rows((4 * POSITIONS, 4 * QUARTER), True)
    for g in range(out_ref.shape[0] // (4 * POSITIONS)):
        rows = slice(g * 4 * POSITIONS, (g + 1) * 4 * POSITIONS)
        short = bs_ref[g * 4 * QUARTER : (g + 1) * 4 * QUARTER, :]
        out_ref[rows, :] = (back[rows] + dot(spread, short)).astype(BF16)


def total_kernel(in_ref, out_ref):
    total = in_ref[0].astype(F32)
    for s in range(1, in_ref.shape[0]):
        total = total + in_ref[s].astype(F32)
    total = total.astype(BF16)
    for d in range(out_ref.shape[0]):
        out_ref[d] = total


def final_kernel(
    scale_in, scale_out, in_ref, gr_ref, gp_ref, ge_ref, gs_ref, gm_ref, sm_ref, gw_ref, sw_ref, sums
):
    def added(devices, rows):
        total = None
        for d in devices:
            part = in_ref[d, rows, :].astype(F32)
            total = part if total is None else total + part
        return total

    count = in_ref.shape[0]
    for core in range(2):
        sums[core * HALF_ROWS : (core + 1) * HALF_ROWS, :] = added(
            range(core, count, 2), slice(0, HALF_ROWS)
        )
    sums[128:144, :] = added(range(count), slice(HALF_ROWS, SUM_ROWS))
    gr_ref[...] = sums[128:144, :] * scale_in
    for j in range(4):
        lanes = slice(j * LANES, (j + 1) * LANES)
        ge_ref[:, lanes] = sums[4 * j : 4 * j + 4, :] * scale_out
        gs_ref[:, lanes] = sums[16 + 16 * j : 32 + 16 * j, :] * scale_out
    share = gp_ref.shape[0]
    gp_ref[...] = sums[80 : 80 + share, :] * scale_out
    line = sums[80 + share : 81 + share, :]

    def gathered(start, per):
        shape = (8, LANES)
        shift = per.bit_length() - 1
        moved = lane_of(shape) - start
        kept = jnp.where(
            (moved >= 0) & ((moved >> shift) == row_of(shape)), jnp.broadcast_to(line, shape), 0.0
        )
        shape = (LANES, per)
        return exact_dot(
            kept, onehot(((row_of(shape) - start) & (per - 1)) == lane_of(shape), F32), ((1,), (0,))
        )

    wide_share = gw_ref.shape[1]
    wide = gathered(0, wide_share) * scale_out
    gw_ref[...] = wide[0:2]
    sw_ref[0:1, :] = wide[2:3]
    sw_ref[1:2, :] = wide[2:3]
    mid = gathered(3 * wide_share, gm_ref.shape[1])
    scales = jnp.where((row_of(mid.shape) & 1) == 0, scale_in, scale_out)
    mid = mid * scales
    gm_ref[...] = mid[2:4]
    sm_ref[...] = mid[0:2]


def step(
    features,
    owners,
    neighbors,
    w_reduce,
    w_spatial,
    w_expand,
    w_short,
    gains_mid,
    shifts_mid,
    gains_wide,
    shifts_wide,
    cotangent,
):
    spaces = lax.axis_size("space")
    dps = lax.axis_size("dp")
    my_index = lax.axis_index("space")
    tiles = features.shape[1]
    width_in = features.shape[3]
    width_mid = w_reduce.shape[1]
    tiles_total = tiles * spaces
    slide_count = features.shape[0] * dps
    capacity = cotangent.shape[1] // spaces
    members_in = float(tiles_total * POSITIONS * (width_mid // GROUPS))
    members_mid = float(tiles_total * QUARTER * (width_mid // GROUPS))
    members_wide = float(tiles_total * QUARTER * (width_in // GROUPS))
    fine, coarse = tiles * POSITIONS, tiles * QUARTER
    stat = struct((spaces, 1, LANES), F32)
    carried = struct((spaces, STAT_ROW + 8, LANES), BF16)
    carried_stat = pl.BlockSpec((spaces, 8, LANES), lambda g: (0, STAT_ROW // 8, 0))
    carried_data = pl.BlockSpec((spaces, STAT_ROW, LANES), lambda g: (0, 0, 0))
    vec_mid, vec_wide = struct((8, width_mid), F32), struct((8, width_in), F32)
    sum_mid, sum_wide = far((8, width_mid), F32), far((8, width_in), F32)
    rims = struct((2 * SIDE, tiles, width_mid), BF16)

    def exchanged(array, axis="space"):
        return lax.all_to_all(array, axis, 0, 0, tiled=True)

    links = neighbors[0]
    links = jnp.where(links >= 0, links - (my_index - 1) * tiles, -1).astype(I32)
    links_across = jnp.pad(links.T, ((0, 5), (0, 0)), constant_values=-1)
    owner_of = owners[0].reshape(tiles)
    core = (lax.axis_index("dp") & 1).reshape(1).astype(I32)
    flat_in = features[0].reshape(fine, width_in)

    steps = 2
    grid_rows = fine // steps
    conv_one, own_rims, stat_one = pl.pallas_call(
        reduce_kernel,
        name="reduce",
        compiler_params=small_grant(),
        grid=(steps,),
        in_specs=[
            pl.BlockSpec((grid_rows, width_in), lambda g: (g, 0)),
            pl.BlockSpec((width_in, width_mid), lambda g: (0, 0)),
            pl.BlockSpec((spaces // steps, capacity * QUARTER, width_in), lambda g: (g, 0, 0)),
        ],
        out_specs=[
            pl.BlockSpec((POSITIONS, tiles // steps, width_mid), lambda g: (0, g, 0)),
            pl.BlockSpec((2 * SIDE, tiles // steps, width_mid), lambda g: (0, g, 0)),
            pl.BlockSpec(carried.shape, lambda g: (0, 0, 0)),
        ],
        out_shape=[far((POSITIONS, tiles, width_mid), BF16), rims, carried],
        scratch_shapes=[pltpu.VMEM((grid_rows, width_mid), F32), pltpu.VMEM((8, width_mid), F32)],
    )(held(flat_in), held(w_reduce), held(cotangent[0].reshape(spaces, capacity * QUARTER, width_in)))
    all_one = exchanged(stat_one)
    prior_rims = lax.ppermute(own_rims, "space", [(i, i + 1) for i in range(spaces - 1)])
    sub_in, conv_short, moments_short = pl.pallas_call(
        short_kernel,
        name="short",
        compiler_params=small_grant(),
        grid=(steps,),
        in_specs=[
            pl.BlockSpec((grid_rows, width_in), lambda g: (g, 0)),
            pl.BlockSpec((width_in, width_in), lambda g: (0, 0)),
        ],
        out_specs=[
            pl.BlockSpec((coarse // steps, width_in), lambda g: (g, 0)),
            pl.BlockSpec((coarse // steps, width_in), lambda g: (g, 0)),
            pl.BlockSpec((8, width_in), lambda g: (0, 0)),
        ],
        out_shape=[
            far((coarse, width_in), BF16),
            struct((coarse, width_in), BF16),
            vec_wide,
        ],
    )(held(flat_in), held(w_short))
    conv_two, columns, vec_one, stat_two = run(
        functools.partial(spatial_kernel, members_in),
        [struct((coarse, width_mid), BF16), far((coarse, 9 * width_mid), BF16), vec_mid, stat],
        (conv_one, prior_rims, all_one, links, gains_mid, shifts_mid, w_spatial),
        [pltpu.VMEM((POSITIONS, tiles, width_mid), BF16)],
        specs={2: carried_stat},
        near=(1, 2, 4, 5, 6),
    )
    all_two = exchanged(stat_two)
    act_two, conv_three, vec_two, stat_wide = run(
        functools.partial(expand_kernel, members_mid),
        [far((coarse, width_mid), BF16), struct((coarse, width_in), BF16), vec_mid, stat],
        (conv_two, all_two, gains_mid, shifts_mid, w_expand, moments_short),
        [pltpu.VMEM((coarse, width_mid), F32)],
        near=(0, 1, 2, 3, 4, 5),
    )
    all_wide = exchanged(stat_wide)
    outgoing, upstream, vec_join, sums_wide = run(
        functools.partial(join_kernel, members_wide, capacity),
        [
            carried,
            far((coarse, width_in), F32),
            vec_wide,
            sum_wide,
        ],
        (owner_of, conv_three, conv_short, all_wide, gains_wide, shifts_wide, all_one),
        [pltpu.SMEM((spaces,), I32), pltpu.SMEM((tiles,), I32)],
        (0,),
        {6: carried_data},
        (1, 2, 3, 4, 5),
    )
    all_back = exchanged(outgoing)
    (block_out,) = run(
        unstack_kernel,
        [far((spaces * capacity, QUARTER, width_in), BF16)],
        (all_back,),
        specs={0: carried_data},
        near=(0,),
    )
    dconv_three, dconv_short, back_two, sums_two, stat_two_back = run(
        functools.partial(back_two_kernel, members_wide),
        [
            far((coarse, width_in), BF16),
            far((coarse, width_in), BF16),
            struct((coarse, width_mid), F32),
            sum_mid,
            stat,
        ],
        (
            conv_three,
            conv_short,
            upstream,
            vec_join,
            all_back,
            gains_wide,
            conv_two,
            vec_two,
            gains_mid,
            shifts_mid,
            w_expand,
        ),
        [pltpu.VMEM((coarse, width_mid), F32)],
        specs={4: carried_stat},
        near=(0, 1, 3, 4, 5, 6, 7, 8, 9, 10),
    )
    all_two_back = exchanged(stat_two_back)
    grad_expand, grad_short, back_short = run(
        wide_grads_kernel,
        [
            far((width_mid, width_in), BF16),
            far((width_in, width_in), BF16),
            far((coarse, width_in), BF16),
        ],
        (act_two, dconv_three, sub_in, dconv_short, w_short),
    )
    dconv_two, back_local, going, sums_one, stat_one_back = run(
        functools.partial(back_one_kernel, members_mid),
        [far((coarse, width_mid), BF16), far((fine, width_mid), F32), rims, sum_mid, stat],
        (
            back_two,
            conv_two,
            vec_two,
            all_two_back,
            gains_mid,
            shifts_mid,
            w_spatial,
            conv_one,
            prior_rims,
            vec_one,
            links_across,
        ),
        [
            pltpu.VMEM((9, QUARTER, tiles, width_mid), F32),
            pltpu.VMEM((2 * SIDE, tiles, width_mid), F32),
        ],
        near=(0, 1, 2, 3, 4, 5, 6, 9, 10),
    )
    all_one_back = exchanged(stat_one_back)
    from_next = lax.ppermute(going, "space", [(i + 1, i) for i in range(spaces - 1)])
    share_spatial = 9 * width_mid // spaces
    halves = [make((spaces, HALF_ROWS, LANES), BF16) for make in (far, struct)]
    keep, send = run(
        mid_grads_kernel,
        halves,
        (core, columns, dconv_two, grad_expand, grad_short, sums_wide, sums_two, sums_one),
        [
            pltpu.VMEM((9 * width_mid, width_mid), F32),
            pltpu.VMEM((spaces, 48, LANES), F32),
            pltpu.VMEM((spaces, 2 * HALF_ROWS, LANES), BF16),
        ],
        (0,),
    )
    twin = lax.ppermute(send, "dp", [(i, i ^ 1) for i in range(dps)])
    dconv_one, outbound = run(
        functools.partial(first_grad_kernel, members_in),
        [far((fine, width_mid), BF16), struct((spaces, SUM_ROWS, LANES), BF16)],
        (back_local, conv_one, from_next, vec_one, all_one_back, gains_mid, shifts_mid, flat_in, keep, twin),
        [pltpu.VMEM((fine, width_mid), F32)],
        near=(2, 3, 4, 5, 6, 9),
    )
    inbound = exchanged(outbound)
    grad_features = pl.pallas_call(
        features_kernel,
        name="featgrad",
        compiler_params=small_grant(),
        grid=(4,),
        in_specs=[
            pl.BlockSpec((fine // 4, width_mid), lambda g: (g, 0)),
            pl.BlockSpec((width_in, width_mid), lambda g: (0, 0)),
            pl.BlockSpec((coarse // 4, width_in), lambda g: (g, 0)),
        ],
        out_specs=pl.BlockSpec((fine // 4, width_in), lambda g: (g, 0)),
        out_shape=far((fine, width_in), BF16),
    )(held(dconv_one), held(w_reduce), held(back_short))
    (mine,) = run(total_kernel, [struct((dps, SUM_ROWS, LANES), BF16)], (inbound,), near=(0,))
    everyone = exchanged(mine, "dp")
    scale_in = 1.0 / math.sqrt(slide_count * tiles_total * POSITIONS)
    scale_out = 1.0 / math.sqrt(slide_count * tiles_total * QUARTER)
    shares = run(
        functools.partial(final_kernel, scale_in, scale_out),
        [
            far((width_in // spaces, width_mid), F32),
            far((share_spatial, width_mid), F32),
            far((width_mid // spaces, width_in), F32),
            far((width_in // spaces, width_in), F32),
            far((2, width_mid // spaces), F32),
            far((2, width_mid // spaces), F32),
            far((2, width_in // spaces), F32),
            far((2, width_in // spaces), F32),
        ],
        (everyone,),
        [pltpu.VMEM((144, LANES), F32)],
        near=(0,),
    )
    return (
        block_out[None],
        grad_features.reshape(1, tiles, POSITIONS, width_in),
        *shares,
    )


def solution(mesh):
    placed = (
        P("dp", "space", None, None),
        P("dp", "space", None),
        P("dp", "space", None),
        P(),
        P(),
        P(),
        P(),
        P(),
        P(),
        P(),
        P(),
        P("dp", "space", None, None),
    )
    return jax.shard_map(
        step,
        mesh=mesh,
        in_specs=placed,
        out_specs=(
            P("dp", "space", None, None),
            P("dp", "space", None, None),
            P("space", None),
            P("space", None),
            P("space", None),
            P("space", None),
            P(None, "space"),
            P(None, "space"),
            P(None, "space"),
            P(None, "space"),
        ),
        check_vma=False,
    )
```
